32 devices in a mesh: row: 8 (over z, core), col: 2 (over y), head: 2 (over x).
Axes of the slice: x: 2, y: 2, z: 4, core: 2. Of those that a mesh axis runs over, the one named last changes fastest.
Arguments:
- x_lo: float32 [6, 32, 64, 4], P('col', 'row', 'head'), may hold values from -32 to 32
- noise: float32 [6, 32, 64, 16], P('col', 'row'), may hold values from -6 to 6
- t_index: int32 [6], P('col'), may hold values from 0 to 999
- labels: int32 [6], P('col'), may hold values from 0 to 1000
- stale_kv: bfloat16 [2, 6, 16, 32, 1152], P(None, 'col', 'row', None, 'head'), may hold values from -6 to 6
- embed_w: float32 [16, 1152], replicated, may hold values from -1.5 to 1.5
- t_w1: bfloat16 [256, 1152], replicated, may hold values from -0.375 to 0.375
- t_w2: bfloat16 [1152, 1152], P(None, 'row'), may hold values from -0.1875 to 0.1875
- class_table: bfloat16 [1001, 1152], P(None, 'row'), may hold values from -6 to 6
- ada_w: bfloat16 [1152, 6912], P('row'), may hold values from -0.1875 to 0.1875
- qkv_w: bfloat16 [1152, 3, 1152], P(None, None, 'head'), may hold values from -0.1875 to 0.1875
- out_w: bfloat16 [1152, 1152], P('head'), may hold values from -0.1875 to 0.1875
- fc1_w: bfloat16 [1152, 4608], P(None, ('col', 'head')), may hold values from -0.1875 to 0.1875
- fc2_w: bfloat16 [1152, 4608], P(None, ('col', 'head')), may hold values from -0.09375 to 0.09375
Outputs:
- tokens_out: bfloat16 [6, 32, 64, 1152], P('col', 'row', 'head')
The draws below stay inside these ranges and needn't reach their ends.
All inputs are finite; a program needn't handle non-finite values.
Results may differ from the reference program's by a relative error of at most 0.025.
Values may be sent and summed in bfloat16 or wider, within the bound.
A program may use at most 128 MiB of HBM per device.

```python
import math
import jax
import jax.numpy as jnp
from jax import lax

HEADS = 16
HD = 72
D = 1152
FF = 4608
NCLASS = 1001
FREQ = 256
C = 4
TSTEPS = 1000
TR = 4
GC = 64
B = 6
GR = 32
LR = 16
LC = 32
N_ROW = 8


def draw_x_lo(key, part):
    subkeys = jax.random.split(key, 4)
    row_values = jnp.arange(GR, dtype=jnp.float32)
    row_scale = jnp.exp(math.log(3.0) * row_values / (GR - 1))
    rough = jnp.exp(jax.random.uniform(subkeys[0], (B, GR, GC, C), minval=math.log(0.5), maxval=math.log(2.0)))
    offset = jax.random.uniform(subkeys[1], (B, 1, 1, C), minval=-1.0, maxval=1.0)
    base_values = jnp.clip(jax.random.normal(subkeys[3], (B, GR, GC, C)), -4.0, 4.0)
    values = base_values * row_scale[None, :, None, None] * rough + offset
    return values.astype(jnp.float32)


def set_ends(values, own_key, least, largest):
    index_at = [jax.random.randint(jax.random.fold_in(own_key, axis), (), 0, length) for axis, length in enumerate(values.shape)]
    longest = values.shape.index(max(values.shape))
    neighbour = index_at[:longest] + [(index_at[longest] + 1) % values.shape[longest]] + index_at[longest + 1:]
    return values.at[tuple(index_at)].set(least).at[tuple(neighbour)].set(largest)


def levels(stream_key, shape, pieces, smallest, high):
    level = 1.0
    for axis_at, blocks in pieces:
        steps = jax.random.uniform(jax.random.fold_in(jax.random.fold_in(stream_key, 6), axis_at), (blocks,), jnp.float32, smallest / len(pieces), high / len(pieces))
        level = level * jnp.repeat(jnp.exp(steps), shape[axis_at] // blocks).reshape((-1,) + (1,) * (len(shape) - 1 - axis_at))
    return level


def gaussian(stream_key, shape, deviation, limit, cuts=(), kind=jnp.bfloat16):
    values = jax.random.normal(stream_key, shape, jnp.float32) * deviation
    if len(cuts) > 0:
        values = levels(stream_key, shape, cuts, -0.22, 0.18) * values
    return jnp.clip(values, min=-limit, max=limit).astype(kind)


def setup_inputs(seed: int = 0) -> dict:
    seeds = jax.random.split(jax.random.key(seed), 15)
    x_lo = draw_x_lo(jax.random.fold_in(seeds[14], 71), 0)
    noise = gaussian(seeds[1], (B, GR, GC, 4 * C), 1.0, 6.0, ((0, 2), (1, 8)), jnp.float32)
    t_index = set_ends(jax.random.randint(seeds[2], (B,), 0, TSTEPS), jax.random.fold_in(seeds[2], 1), 0, TSTEPS - 1).astype(jnp.int32)
    labels = set_ends(jax.random.randint(seeds[3], (B,), 0, NCLASS), jax.random.fold_in(seeds[3], 1), 0, NCLASS - 1).astype(jnp.int32)
    stale_kv = gaussian(seeds[4], (2, B, LR, LC, D), 1.0, 6.0, ((1, 2), (2, 8), (4, 2)))
    embed_w = gaussian(seeds[5], (4 * C, D), (4 * C) ** -0.5, 1.5, (), jnp.float32)
    t_w1 = gaussian(seeds[6], (FREQ, D), FREQ ** -0.5, 0.375)
    t_w2 = gaussian(seeds[7], (D, D), D ** -0.5, 0.1875, ((1, 8),))
    class_table = gaussian(seeds[8], (NCLASS, D), 1.0, 6.0, ((1, 8),))
    ada_w = gaussian(seeds[9], (D, 6 * D), D ** -0.5, 0.1875, ((0, 8),))
    qkv_w = gaussian(seeds[10], (D, 3, D), D ** -0.5, 0.1875, ((2, 2),))
    out_w = gaussian(seeds[11], (D, D), D ** -0.5, 0.1875, ((0, 2),))
    fc1_w = gaussian(seeds[12], (D, FF), D ** -0.5, 0.1875, ((1, 4),))
    fc2_w = gaussian(seeds[13], (D, FF), FF ** -0.5, 0.09375, ((1, 4),))
    return dict(x_lo=x_lo, noise=noise, t_index=t_index, labels=labels, stale_kv=stale_kv, embed_w=embed_w, t_w1=t_w1, t_w2=t_w2, class_table=class_table, ada_w=ada_w, qkv_w=qkv_w, out_w=out_w, fc1_w=fc1_w, fc2_w=fc2_w)


def upsample_padded(padded):
    upper = padded[:, :-2]
    middle = padded[:, 1:-1]
    lower = padded[:, 2:]
    rows_even = 0.75 * middle + 0.25 * upper
    rows_odd = 0.75 * middle + 0.25 * lower

    def widen(vertical):
        left_side = vertical[:, :, :-2]
        centre = vertical[:, :, 1:-1]
        right_side = vertical[:, :, 2:]
        return jnp.stack([0.75 * centre + 0.25 * left_side, 0.75 * centre + 0.25 * right_side], axis=3)
    stacked = jnp.stack([widen(rows_even), widen(rows_odd)], axis=3)
    return stacked.reshape(stacked.shape[0], stacked.shape[1], stacked.shape[2], 4 * stacked.shape[-1])

def noise_level(t_index):
    step_values = jnp.arange(TSTEPS, dtype=jnp.float32)
    betas = 0.0001 + (0.02 - 0.0001) * step_values / (TSTEPS - 1)
    log_keep = jnp.cumsum(jnp.log(1.0 - betas))
    picked = (jnp.arange(TSTEPS, dtype=jnp.int32)[None, :] == t_index[:, None]).astype(jnp.float32)
    return jnp.exp(lax.optimization_barrier(jnp.sum(picked * log_keep[None, :], axis=1)))

def position_table(row_pos, col_pos, width):
    quarter = width // 4
    omega = 1.0 / 10000.0 ** (jnp.arange(quarter, dtype=jnp.float32) / quarter)
    row_args = row_pos[:, None] * omega[None, :]
    col_args = col_pos[:, None] * omega[None, :]
    row_part = jnp.concatenate([jnp.sin(row_args), jnp.cos(row_args)], axis=1)
    col_part = jnp.concatenate([jnp.sin(col_args), jnp.cos(col_args)], axis=1)
    n_rows = row_pos.shape[0]
    n_cols = col_pos.shape[0]
    return jnp.concatenate([jnp.broadcast_to(row_part[:, None, :], (n_rows, n_cols, width // 2)), jnp.broadcast_to(col_part[None, :, :], (n_rows, n_cols, width // 2))], axis=2)

def condition(t_index, labels, t_w1, t_w2, class_table):
    half_freq = t_w1.shape[0] // 2
    freqs = jnp.exp(-math.log(10000.0) * jnp.arange(half_freq, dtype=jnp.float32) / half_freq)
    angles = t_index.astype(jnp.float32)[:, None] * freqs[None, :]
    freq_feat = jnp.concatenate([jnp.cos(angles), jnp.sin(angles)], axis=1).astype(jnp.bfloat16)
    t_hidden = jax.nn.silu(jnp.dot(freq_feat, t_w1, preferred_element_type=jnp.float32)).astype(jnp.bfloat16)
    t_embed = jnp.dot(t_hidden, t_w2, preferred_element_type=jnp.float32)
    onehot = (jnp.arange(class_table.shape[0], dtype=jnp.int32)[None, :] == labels[:, None]).astype(jnp.bfloat16)
    return t_embed + jnp.dot(onehot, class_table, preferred_element_type=jnp.float32)

def layer_norm(values):
    centre = lax.optimization_barrier(jnp.mean(values, axis=-1, keepdims=True))
    spread = lax.optimization_barrier(jnp.mean((values - centre) ** 2, axis=-1, keepdims=True))
    return (values - centre) * lax.rsqrt(spread + 1e-06)

def attend_image(operands):
    query, key, value, stale_key, stale_value = operands
    n_patch = N_ROW
    per_patch = TR * GC

    def to_patches(tensor):
        return tensor.reshape(n_patch, per_patch, HEADS, HD).astype(jnp.float32)
    query_p = to_patches(query)
    key_p = to_patches(key)
    value_p = to_patches(value)
    coarse_key = stale_key.reshape(LR * LC, HEADS, HD).astype(jnp.float32)
    coarse_value = stale_value.reshape(LR * LC, HEADS, HD).astype(jnp.float32)
    scale = 1.0 / math.sqrt(HD)
    fresh = jnp.einsum('pqhd,pkhd->phqk', query_p, key_p) * scale
    stale = jnp.einsum('pqhd,khd->phqk', query_p, coarse_key) * scale + math.log(4.0)
    key_patch = jnp.broadcast_to((jnp.arange(LR, dtype=jnp.int32) // (TR // 2))[:, None], (LR, LC)).reshape(LR * LC)
    own = key_patch[None, :] == jnp.arange(n_patch, dtype=jnp.int32)[:, None]
    stale = jnp.where(own[:, None, None, :], jnp.float32(-1e+30), stale)
    scores = jnp.concatenate([fresh, stale], axis=-1)
    weights = jax.nn.softmax(scores, axis=-1).astype(jnp.bfloat16).astype(jnp.float32)
    attended = jnp.einsum('phqk,pkhd->pqhd', weights[..., :per_patch], value_p)
    attended = attended + jnp.einsum('phqk,khd->pqhd', weights[..., per_patch:], coarse_value)
    return attended.reshape(GR, GC, HEADS * HD).astype(jnp.bfloat16)

def reference(x_lo, noise, t_index, labels, stale_kv, embed_w, t_w1, t_w2, class_table, ada_w, qkv_w, out_w, fc1_w, fc2_w):
    abar = noise_level(t_index)
    padded = jnp.pad(x_lo, ((0, 0), (1, 1), (1, 1), (0, 0)), mode='edge')
    upsampled = upsample_padded(padded)
    noisy = jnp.sqrt(abar)[:, None, None, None] * upsampled + jnp.sqrt(1.0 - abar)[:, None, None, None] * noise
    grouped = noisy.reshape(B, GR, GC, 4, C)
    count = 4.0 * GR * GC
    total = lax.optimization_barrier(jnp.sum(grouped, axis=(1, 2, 3)))
    squares = lax.optimization_barrier(jnp.sum(grouped * grouped, axis=(1, 2, 3)))
    centre = total / count
    spread = squares / count - centre * centre
    normed = ((grouped - centre[:, None, None, None, :]) * lax.rsqrt(spread + 1e-05)[:, None, None, None, :]).reshape(B, GR, GC, 4 * C)
    pos = position_table(jnp.arange(GR, dtype=jnp.float32), jnp.arange(GC, dtype=jnp.float32), D)
    tokens = (jnp.einsum('bijf,fd->bijd', normed, embed_w, precision=lax.Precision.HIGHEST) + pos[None]).astype(jnp.bfloat16)
    cond = condition(t_index, labels, t_w1, t_w2, class_table)
    cond_act = jax.nn.silu(cond).astype(jnp.bfloat16)
    modulation = jnp.dot(cond_act, ada_w, preferred_element_type=jnp.float32)
    shift1, scale1, gate1, shift2, scale2, gate2 = jnp.split(modulation, 6, axis=1)
    flat = tokens.astype(jnp.float32).reshape(B, GR * GC, D)
    normed1 = (layer_norm(flat) * (1.0 + scale1[:, None, :]) + shift1[:, None, :]).astype(jnp.bfloat16)
    qkv = jnp.dot(normed1.reshape(B * GR * GC, D), qkv_w.reshape(D, 3 * D), preferred_element_type=jnp.float32)
    qkv = qkv.astype(jnp.bfloat16).reshape(B, GR, GC, 3, HEADS, HD)
    stale = stale_kv.reshape(2, B, LR, LC, HEADS, HD)
    attended = lax.map(attend_image, (qkv[:, :, :, 0], qkv[:, :, :, 1], qkv[:, :, :, 2], stale[0], stale[1]))
    projected = jnp.dot(attended.reshape(B * GR * GC, D), out_w, preferred_element_type=jnp.float32).reshape(B, GR * GC, D)
    mid = (flat + gate1[:, None, :] * projected).astype(jnp.bfloat16)
    normed2 = (layer_norm(mid.astype(jnp.float32)) * (1.0 + scale2[:, None, :]) + shift2[:, None, :]).astype(jnp.bfloat16)
    hidden = jax.nn.gelu(jnp.dot(normed2.reshape(B * GR * GC, D), fc1_w, preferred_element_type=jnp.float32), approximate=True).astype(jnp.bfloat16)
    mlp_term = lax.dot_general(hidden, fc2_w, (((1,), (1,)), ((), ())), preferred_element_type=jnp.float32).reshape(B, GR * GC, D)
    tokens_out = (mid.astype(jnp.float32) + gate2[:, None, :] * mlp_term).astype(jnp.bfloat16)
    return tokens_out.reshape(B, GR, GC, D)
```

```python
import functools
import math

import jax
import jax.numpy as jnp
from jax import lax
from jax.experimental import pallas as pl
from jax.experimental.pallas import tpu as pltpu
from jax.sharding import PartitionSpec as P

HD = 72
TSTEPS = 1000


def upsample_padded(padded):
    upper = padded[:, :-2]
    middle = padded[:, 1:-1]
    lower = padded[:, 2:]
    rows_even = 0.75 * middle + 0.25 * upper
    rows_odd = 0.75 * middle + 0.25 * lower

    def widen(vertical):
        left_side = vertical[:, :, :-2]
        centre = vertical[:, :, 1:-1]
        right_side = vertical[:, :, 2:]
        return jnp.stack(
            [0.75 * centre + 0.25 * left_side, 0.75 * centre + 0.25 * right_side], axis=3
        )

    stacked = jnp.stack([widen(rows_even), widen(rows_odd)], axis=3)
    return stacked.reshape(
        stacked.shape[0], stacked.shape[1], stacked.shape[2], 4 * stacked.shape[-1]
    )


def clamp_edges(padded, axis_dim, at_start, at_end):
    length = padded.shape[axis_dim]
    leading = lax.slice_in_dim(padded, 0, 1, axis=axis_dim)
    second_row = lax.slice_in_dim(padded, 1, 2, axis=axis_dim)
    trailing = lax.slice_in_dim(padded, length - 1, length, axis=axis_dim)
    before_end = lax.slice_in_dim(padded, length - 2, length - 1, axis=axis_dim)
    leading = jnp.where(at_start, second_row, leading)
    trailing = jnp.where(at_end, before_end, trailing)
    return jnp.concatenate(
        [leading, lax.slice_in_dim(padded, 1, length - 1, axis=axis_dim), trailing], axis=axis_dim
    )


def noise_level(t_index):
    step_values = jnp.arange(TSTEPS, dtype=jnp.float32)
    betas = 0.0001 + (0.02 - 0.0001) * step_values / (TSTEPS - 1)
    log_keep = jnp.cumsum(jnp.log(1.0 - betas))
    picked = (jnp.arange(TSTEPS, dtype=jnp.int32)[None, :] == t_index[:, None]).astype(jnp.float32)
    return jnp.exp(jnp.sum(picked * log_keep[None, :], axis=1))


def position_table(row_pos, col_pos, width):
    quarter = width // 4
    omega = 1.0 / 10000.0 ** (jnp.arange(quarter, dtype=jnp.float32) / quarter)
    row_args = row_pos[:, None] * omega[None, :]
    col_args = col_pos[:, None] * omega[None, :]
    row_part = jnp.concatenate([jnp.sin(row_args), jnp.cos(row_args)], axis=1)
    col_part = jnp.concatenate([jnp.sin(col_args), jnp.cos(col_args)], axis=1)
    n_rows = row_pos.shape[0]
    n_cols = col_pos.shape[0]
    return jnp.concatenate(
        [
            jnp.broadcast_to(row_part[:, None, :], (n_rows, n_cols, width // 2)),
            jnp.broadcast_to(col_part[None, :, :], (n_rows, n_cols, width // 2)),
        ],
        axis=2,
    )


def condition(t_index, labels, t_w1, t_w2, class_table):
    half_freq = t_w1.shape[0] // 2
    freqs = jnp.exp(-math.log(10000.0) * jnp.arange(half_freq, dtype=jnp.float32) / half_freq)
    angles = t_index.astype(jnp.float32)[:, None] * freqs[None, :]
    freq_feat = jnp.concatenate([jnp.cos(angles), jnp.sin(angles)], axis=1).astype(jnp.bfloat16)
    t_hidden = jax.nn.silu(jnp.dot(freq_feat, t_w1, preferred_element_type=jnp.float32)).astype(
        jnp.bfloat16
    )
    t_embed = jnp.dot(t_hidden, t_w2, preferred_element_type=jnp.float32)
    onehot = (jnp.arange(class_table.shape[0], dtype=jnp.int32)[None, :] == labels[:, None]).astype(
        jnp.bfloat16
    )
    return t_embed + jnp.dot(onehot, class_table, preferred_element_type=jnp.float32)


def layer_norm(values):
    centre = jnp.mean(values, axis=-1, keepdims=True)
    spread = jnp.mean((values - centre) ** 2, axis=-1, keepdims=True)
    return (values - centre) * lax.rsqrt(spread + 1e-06)


def spread_out(vector):
    return vector[:, None, None, :]


MESH = pl.DeviceIdType.MESH
VMEM_LIMIT = 60 * 1024 * 1024


def vmem():
    return pl.BlockSpec(memory_space=pltpu.VMEM)


def anywhere():
    return pl.BlockSpec(memory_space=pl.ANY)


def greet(peers):
    barrier = pltpu.get_barrier_semaphore()
    for peer in peers:
        pl.semaphore_signal(barrier, inc=1, device_id=peer, device_id_type=MESH)
    pl.semaphore_wait(barrier, len(peers))


def remote(src, dst, send, recv, peer):
    return pltpu.make_async_remote_copy(
        src_ref=src, dst_ref=dst, send_sem=send, recv_sem=recv, device_id=peer, device_id_type=MESH
    )


def halo_kernel(n, x_ref, out_ref, got, send, recv):
    row = lax.axis_index("row")
    other = 1 - lax.axis_index("head")
    above = lax.rem(row + n - 1, n)
    below = lax.rem(row + 1, n)
    plan = [
        ({"row": above}, 4),
        ({"row": above, "head": other}, 5),
        ({"head": other}, 3),
        ({"row": below}, 0),
        ({"row": below, "head": other}, 1),
    ]
    greet([peer for peer, _ in plan])
    copies = [
        remote(x_ref, got.at[slot], send.at[slot], recv.at[slot], peer) for peer, slot in plan
    ]
    for copy in copies:
        copy.start()
    out_ref[2] = x_ref[...]
    for copy, (_, slot) in zip(copies, plan):
        copy.wait()
        out_ref[slot] = got[slot]


def halo_exchange(block, n):
    rows, lanes = block.shape
    return pl.pallas_call(
        functools.partial(halo_kernel, n),
        out_shape=jax.ShapeDtypeStruct((6, rows, lanes), block.dtype),
        in_specs=[vmem()],
        out_specs=vmem(),
        scratch_shapes=[
            pltpu.VMEM((6, rows, lanes), block.dtype),
            pltpu.SemaphoreType.DMA((6,)),
            pltpu.SemaphoreType.DMA((6,)),
        ],
        compiler_params=pltpu.CompilerParams(collective_id=1, has_side_effects=True),
        name="halo",
    )(block)


def sums_kernel(n, s_ref, m_ref, s_out, m_out, s_got, m_got, s_send, s_recv, m_send, m_recv):
    row = lax.axis_index("row")
    peers = [{"row": lax.rem(row + k, n)} for k in range(1, n)]
    greet(peers)
    copies = []
    for k, peer in enumerate(peers):
        copies.append(remote(s_ref, s_got.at[k], s_send.at[k], s_recv.at[k], peer))
        copies.append(remote(m_ref, m_got.at[k], m_send.at[k], m_recv.at[k], peer))
    for copy in copies:
        copy.start()
    for copy in copies:
        copy.wait()
    stats = s_ref[...]
    parts = m_ref[...].astype(jnp.float32)
    for k in range(n - 1):
        stats = stats + s_got[k]
        parts = parts + m_got[k].astype(jnp.float32)
    s_out[...] = stats
    m_out[...] = parts


def row_sums(stats, parts, n):
    return pl.pallas_call(
        functools.partial(sums_kernel, n),
        out_shape=(
            jax.ShapeDtypeStruct(stats.shape, jnp.float32),
            jax.ShapeDtypeStruct(parts.shape, jnp.float32),
        ),
        in_specs=[vmem()] * 2,
        out_specs=(vmem(), vmem()),
        scratch_shapes=[
            pltpu.VMEM((n - 1,) + stats.shape, stats.dtype),
            pltpu.VMEM((n - 1,) + parts.shape, parts.dtype),
        ]
        + [pltpu.SemaphoreType.DMA((n - 1,))] * 4,
        compiler_params=pltpu.CompilerParams(collective_id=2, has_side_effects=True),
        name="row_sums",
    )(stats, parts)


def dot_nt(left, right):
    return lax.dot_general(left, right, (((1,), (1,)), ((), ())), preferred_element_type=jnp.float32)


def dot_nn(left, right):
    return jnp.dot(left, right, preferred_element_type=jnp.float32)


def attention_kernel(pieces, q_ref, k_ref, v_ref, tok_ref, mod_ref, ow_ref, *rest):
    stale = rest[:pieces]
    mid_ref, n2_ref = rest[pieces : pieces + 2]
    kv, acc, part, got, l_sem, s_sem, r_sem, ps_sem, pr_sem = rest[pieces + 2 :]
    batch, tokens, local_width = q_ref.shape
    tile_rows, full_cols, width = tok_ref.shape[1:]
    half = full_cols // 2
    keys = stale[0].shape[2]
    row = lax.axis_index("row")
    head = lax.axis_index("head")
    twin = {"row": row + 1 - 2 * lax.rem(row, 2)}
    other = {"head": 1 - head}
    greet([twin, other])

    def stale_copies(b):
        copies = []
        for i in range(1, pieces):
            copies.append(
                pltpu.make_async_copy(
                    stale[i].at[:, b], kv.at[:, b, pl.ds((i - 1) * keys, keys)], l_sem.at[b, i]
                )
            )
        for i in range(pieces):
            copies.append(
                remote(
                    stale[i].at[:, b],
                    kv.at[:, b, pl.ds((pieces - 1 + i) * keys, keys)],
                    s_sem.at[b, i],
                    r_sem.at[b, i],
                    twin,
                )
            )
        return copies

    def part_copy(b):
        return remote(
            part.at[b, :, pl.ds(pl.multiple_of((1 - head) * half, half), half)],
            got.at[b],
            ps_sem.at[b],
            pr_sem.at[b],
            other,
        )

    @pl.loop(0, batch)
    def _(b):
        for copy in stale_copies(b):
            copy.start()

    acc[...] = jnp.zeros_like(acc)

    @pl.loop(0, batch)
    def _(b):
        for copy in stale_copies(b):
            copy.wait()
        for h in range(local_width // HD):
            low, high = h * HD, (h + 1) * HD
            first = low // 128 * 128
            last = min(-(-high // 128) * 128, local_width)
            lanes = lax.broadcasted_iota(jnp.int32, (1, last - first), 1) + first
            inside = (lanes >= low) & (lanes < high)
            keep = jnp.where(inside, 1.0, 0.0)
            query = q_ref[b, :, first:last] * keep.astype(jnp.bfloat16)
            fresh = dot_nt(query, k_ref[b, :, first:last])
            coarse = dot_nt(query, kv[0, b, :, first:last]) + 2.0
            top = jnp.maximum(
                jnp.max(fresh, axis=1, keepdims=True), jnp.max(coarse, axis=1, keepdims=True)
            )
            fresh = jnp.exp2(fresh - top)
            coarse = jnp.exp2(coarse - top)
            mass = jnp.sum(fresh, axis=1, keepdims=True) + jnp.sum(coarse, axis=1, keepdims=True)
            mixed = dot_nn(fresh.astype(jnp.bfloat16), v_ref[b, :, first:last]) + dot_nn(
                coarse.astype(jnp.bfloat16), kv[1, b, :, first:last]
            )
            mixed = mixed * (1.0 / mass)
            acc[:, first:last] = jnp.where(inside, mixed, acc[:, first:last])
        proj = dot_nn(acc[...].astype(jnp.bfloat16), ow_ref[...])
        part[b] = proj.reshape(tile_rows, full_cols, width).astype(jnp.bfloat16)
        part_copy(b).start()

    mine = pl.ds(pl.multiple_of(head * half, half), half)

    @pl.loop(0, batch)
    def _(b):
        part_copy(b).wait()
        total = part[b, :, mine].astype(jnp.float32) + got[b].astype(jnp.float32)
        total = total.reshape(tile_rows * half, width)
        tok = tok_ref[b, :, mine].astype(jnp.float32).reshape(tile_rows * half, width)
        mod = mod_ref[b]
        mid = (tok + mod[2:3] * total).astype(jnp.bfloat16)
        mid_ref[b] = mid
        n2_ref[b] = (
            layer_norm(mid.astype(jnp.float32)) * (1.0 + mod[4:5]) + mod[3:4]
        ).astype(jnp.bfloat16)


def attention_block(query, key, value, tokens, mod, out_w, stale):
    batch, tile_rows, full_cols, width = tokens.shape
    local_width = query.shape[2]
    pieces = len(stale)
    keys = stale[0].shape[2]
    half = full_cols // 2
    out = jax.ShapeDtypeStruct((batch, tile_rows * half, width), jnp.bfloat16)
    return pl.pallas_call(
        functools.partial(attention_kernel, pieces),
        out_shape=(out, out),
        in_specs=[vmem()] * 6 + [anywhere()] * pieces,
        out_specs=(vmem(), vmem()),
        scratch_shapes=[
            pltpu.VMEM((2, batch, (2 * pieces - 1) * keys, local_width), jnp.bfloat16),
            pltpu.VMEM((tile_rows * full_cols, local_width), jnp.float32),
            pltpu.VMEM((batch, tile_rows, full_cols, width), jnp.bfloat16),
            pltpu.VMEM((batch, tile_rows, half, width), jnp.bfloat16),
            pltpu.SemaphoreType.DMA((batch, pieces)),
            pltpu.SemaphoreType.DMA((batch, pieces)),
            pltpu.SemaphoreType.DMA((batch, pieces)),
            pltpu.SemaphoreType.DMA((batch,)),
            pltpu.SemaphoreType.DMA((batch,)),
        ],
        compiler_params=pltpu.CompilerParams(
            collective_id=3, has_side_effects=True, vmem_limit_bytes=VMEM_LIMIT
        ),
        name="attention",
    )(query, key, value, tokens, mod, out_w, *stale)


def mlp_kernel(far, n2_ref, mid_ref, mod_ref, up_ref, down_ref, *rest):
    ups = rest[:far]
    downs = rest[far : 2 * far]
    out_ref = rest[2 * far]
    n2_got, ups_all, downs_all, own, part, got, ns, nr, ps, pr, wl, ws, wr = rest[2 * far + 1 :]
    batch, tokens, width = n2_ref.shape
    rows = ups[0].shape[0]
    row = lax.axis_index("row")
    core = lax.rem(row, 2)
    twin = {"row": row + 1 - 2 * core}
    other = {"head": 1 - lax.axis_index("head")}
    greet([twin, other])

    def token_copy(b):
        return remote(n2_ref.at[b], n2_got.at[b], ns.at[b], nr.at[b], other)

    def part_copy(b):
        return remote(part.at[b], got.at[b], ps.at[b], pr.at[b], other)

    at = pl.ds(pl.multiple_of(core * rows, rows), rows)
    weight_copies = []
    for i in range(far):
        for j, (source, target) in enumerate(((ups[i], ups_all), (downs[i], downs_all))):
            place = target.at[i, at]
            weight_copies.append(pltpu.make_async_copy(source, place, wl.at[i, j]))
            weight_copies.append(remote(source, place, ws.at[i, j], wr.at[i, j], twin))

    for b in range(batch):
        token_copy(b).start()
    for copy in weight_copies:
        copy.start()

    def mlp(rows_in, up, down):
        hidden = jax.nn.gelu(dot_nn(rows_in, up), approximate=True).astype(jnp.bfloat16)
        return dot_nt(hidden, down)

    flat = n2_ref[...].reshape(batch * tokens, width)
    own[...] = mlp(flat, up_ref[...], down_ref[...]).reshape(own.shape)
    for copy in weight_copies:
        copy.wait()

    @pl.loop(0, far)
    def _(i):
        flat = n2_ref[...].reshape(batch * tokens, width)
        own[...] += mlp(flat, ups_all[i], downs_all[i]).reshape(own.shape)

    @pl.loop(0, batch)
    def _(b):
        token_copy(b).wait()
        theirs = n2_got[b]
        total = mlp(theirs, up_ref[...], down_ref[...])
        total = lax.fori_loop(
            0, far, lambda i, so_far: so_far + mlp(theirs, ups_all[i], downs_all[i]), total
        )
        part[b] = total.astype(jnp.bfloat16)
        part_copy(b).start()

    @pl.loop(0, batch)
    def _(b):
        part_copy(b).wait()
        total = own[b] + got[b].astype(jnp.float32)
        gate = mod_ref[b][5:6]
        out_ref[b] = (mid_ref[b].astype(jnp.float32) + gate * total).astype(jnp.bfloat16)


def mlp_block(n2, mid, mod, up, down, ups, downs):
    far = len(ups)
    batch, tokens, width = n2.shape
    hidden = up.shape[1]
    return pl.pallas_call(
        functools.partial(mlp_kernel, far),
        out_shape=jax.ShapeDtypeStruct(n2.shape, jnp.bfloat16),
        in_specs=[vmem()] * 5 + [anywhere()] * (2 * far),
        out_specs=vmem(),
        scratch_shapes=[
            pltpu.VMEM(n2.shape, jnp.bfloat16),
            pltpu.VMEM((far, width, hidden), jnp.bfloat16),
            pltpu.VMEM((far, width, hidden), jnp.bfloat16),
            pltpu.VMEM(n2.shape, jnp.float32),
            pltpu.VMEM(n2.shape, jnp.bfloat16),
            pltpu.VMEM(n2.shape, jnp.bfloat16),
        ]
        + [pltpu.SemaphoreType.DMA((batch,))] * 4
        + [pltpu.SemaphoreType.DMA((far, 2))] * 3,
        compiler_params=pltpu.CompilerParams(
            collective_id=4, has_side_effects=True, vmem_limit_bytes=VMEM_LIMIT
        ),
        name="mlp",
    )(n2, mid, mod, up, down, *ups, *downs)


def shifted(block, axis, step):
    count = lax.axis_size(axis)
    return lax.ppermute(block, axis, [(i, (i + step) % count) for i in range(count)])


def body(
    x_lo,
    noise,
    t_index,
    labels,
    stale_kv,
    embed_w,
    t_w1,
    t_w2,
    class_table,
    ada_w,
    qkv_w,
    out_w,
    fc1_w,
    fc2_w,
):
    row_index = lax.axis_index("row")
    row_count = lax.axis_size("row")
    head_index = lax.axis_index("head")
    head_count = lax.axis_size("head")
    batch = noise.shape[0]
    tile_rows = noise.shape[1]
    full_cols = noise.shape[2]
    channels = x_lo.shape[3]
    width = embed_w.shape[1]
    local_width = qkv_w.shape[2]
    stale_local = stale_kv.reshape(2, batch, -1, local_width)
    stale = [stale_local]
    stale += [shifted(stale_local, "row", 2 * k) for k in range(1, row_count // 2)]
    core = lax.rem(row_index, 2)
    rows = fc1_w.shape[0] // 2
    up_half = lax.dynamic_slice_in_dim(fc1_w, core * rows, rows, 0)
    down_half = lax.dynamic_slice_in_dim(fc2_w, core * rows, rows, 0)
    ups = [shifted(up_half, "col", k) for k in range(1, lax.axis_size("col"))]
    downs = [shifted(down_half, "col", k) for k in range(1, lax.axis_size("col"))]
    abar = noise_level(t_index)
    half_cols = full_cols // head_count
    slots = halo_exchange(x_lo.reshape(batch * tile_rows, half_cols * channels), row_count)
    slots = slots.reshape(3, 2, batch, tile_rows, half_cols, channels)
    left = jnp.where(head_index == 0, slots[:, 0], slots[:, 1])
    right = jnp.where(head_index == 0, slots[:, 1], slots[:, 0])
    gathered = jnp.concatenate([left, right], axis=3)
    padded = jnp.concatenate([gathered[0][:, -1:], gathered[1], gathered[2][:, :1]], axis=1)
    padded = clamp_edges(padded, 1, row_index == 0, row_index == row_count - 1)
    padded = jnp.pad(padded, ((0, 0), (0, 0), (1, 1), (0, 0)), mode="edge")
    upsampled = upsample_padded(padded)
    noisy = (
        jnp.sqrt(abar)[:, None, None, None] * upsampled
        + jnp.sqrt(1.0 - abar)[:, None, None, None] * noise
    )
    grouped = noisy.reshape(batch, tile_rows, full_cols, 4, channels)
    cond_part = condition(t_index, labels, t_w1, t_w2, class_table)
    cond_act = jax.nn.silu(cond_part).astype(jnp.bfloat16)
    mod_part = jnp.dot(cond_act, ada_w, preferred_element_type=jnp.float32).astype(jnp.bfloat16)
    sums = jnp.concatenate(
        [
            jnp.sum(grouped, axis=(1, 2, 3)).reshape(-1),
            jnp.sum(grouped * grouped, axis=(1, 2, 3)).reshape(-1),
        ]
    )
    n_sums = sums.shape[0]
    sums = jnp.broadcast_to(jnp.pad(sums, (0, 128 - n_sums))[None], (8, 128))
    sums, modulation = row_sums(sums, mod_part.reshape(-1, 128), row_count)
    total, squares = sums[0, :n_sums].reshape(2, batch, channels)
    modulation = modulation.reshape(batch, 6, width)
    count = 4.0 * tile_rows * row_count * full_cols
    centre = total / count
    spread = squares / count - centre * centre
    normed = (
        (grouped - centre[:, None, None, None, :])
        * lax.rsqrt(spread + 1e-05)[:, None, None, None, :]
    ).reshape(batch, tile_rows, full_cols, 4 * channels)
    row_pos = (row_index * tile_rows + jnp.arange(tile_rows, dtype=jnp.int32)).astype(jnp.float32)
    col_pos = jnp.arange(full_cols, dtype=jnp.float32)
    pos = position_table(row_pos, col_pos, width)
    tokens = (
        jnp.einsum("bijf,fd->bijd", normed, embed_w, precision=lax.Precision.HIGHEST) + pos[None]
    ).astype(jnp.bfloat16)
    shift1 = modulation[:, 0]
    scale1 = modulation[:, 1]
    per_image = tile_rows * full_cols
    flat = tokens.astype(jnp.float32)
    normed1 = (layer_norm(flat) * (1.0 + spread_out(scale1)) + spread_out(shift1)).astype(
        jnp.bfloat16
    )
    rows_in = normed1.reshape(batch * per_image, width)
    scale = math.log2(math.e) / math.sqrt(HD)

    def project(which):
        return jnp.dot(rows_in, qkv_w[:, which], preferred_element_type=jnp.float32)

    query = (project(0) * scale).astype(jnp.bfloat16).reshape(batch, per_image, local_width)
    key = project(1).astype(jnp.bfloat16).reshape(batch, per_image, local_width)
    value = project(2).astype(jnp.bfloat16).reshape(batch, per_image, local_width)
    mid, normed2 = attention_block(query, key, value, tokens, modulation, out_w, stale)
    tokens_out = mlp_block(normed2, mid, modulation, fc1_w, fc2_w, ups, downs)
    return tokens_out.reshape(batch, tile_rows, half_cols, width)


def solution(mesh):
    placed = (
        P("col", "row", "head", None),
        P("col", "row", None, None),
        P("col"),
        P("col"),
        P(None, "col", "row", None, "head"),
        P(),
        P(),
        P(None, "row"),
        P(None, "row"),
        P("row", None),
        P(None, None, "head"),
        P("head", None),
        P(None, ("col", "head")),
        P(None, ("col", "head")),
    )
    return jax.shard_map(
        body, mesh=mesh, in_specs=placed, out_specs=P("col", "row", "head", None), check_vma=False
    )
```

```python
import functools
import math

import jax
import jax.numpy as jnp
from jax import lax
from jax.experimental import pallas as pl
from jax.experimental.pallas import tpu as pltpu
from jax.sharding import PartitionSpec as P

HD = 72
TSTEPS = 1000


def upsample_padded(padded):
    upper = padded[:, :-2]
    middle = padded[:, 1:-1]
    lower = padded[:, 2:]
    rows_even = 0.75 * middle + 0.25 * upper
    rows_odd = 0.75 * middle + 0.25 * lower

    def widen(vertical):
        left_side = vertical[:, :, :-2]
        centre = vertical[:, :, 1:-1]
        right_side = vertical[:, :, 2:]
        return jnp.stack(
            [0.75 * centre + 0.25 * left_side, 0.75 * centre + 0.25 * right_side], axis=3
        )

    stacked = jnp.stack([widen(rows_even), widen(rows_odd)], axis=3)
    return stacked.reshape(
        stacked.shape[0], stacked.shape[1], stacked.shape[2], 4 * stacked.shape[-1]
    )


def noise_level(t_index):
    step_values = jnp.arange(TSTEPS, dtype=jnp.float32)
    betas = 0.0001 + (0.02 - 0.0001) * step_values / (TSTEPS - 1)
    log_keep = jnp.cumsum(jnp.log(1.0 - betas))
    picked = (jnp.arange(TSTEPS, dtype=jnp.int32)[None, :] == t_index[:, None]).astype(jnp.float32)
    return jnp.exp(jnp.sum(picked * log_keep[None, :], axis=1))


def position_table(row_pos, col_pos, width):
    quarter = width // 4
    omega = 1.0 / 10000.0 ** (jnp.arange(quarter, dtype=jnp.float32) / quarter)
    row_args = row_pos[:, None] * omega[None, :]
    col_args = col_pos[:, None] * omega[None, :]
    row_part = jnp.concatenate([jnp.sin(row_args), jnp.cos(row_args)], axis=1)
    col_part = jnp.concatenate([jnp.sin(col_args), jnp.cos(col_args)], axis=1)
    n_rows = row_pos.shape[0]
    n_cols = col_pos.shape[0]
    return jnp.concatenate(
        [
            jnp.broadcast_to(row_part[:, None, :], (n_rows, n_cols, width // 2)),
            jnp.broadcast_to(col_part[None, :, :], (n_rows, n_cols, width // 2)),
        ],
        axis=2,
    )


def condition(t_index, labels, t_w1, t_w2, class_table):
    half_freq = t_w1.shape[0] // 2
    freqs = jnp.exp(-math.log(10000.0) * jnp.arange(half_freq, dtype=jnp.float32) / half_freq)
    angles = t_index.astype(jnp.float32)[:, None] * freqs[None, :]
    freq_feat = jnp.concatenate([jnp.cos(angles), jnp.sin(angles)], axis=1).astype(jnp.bfloat16)
    t_hidden = jax.nn.silu(jnp.dot(freq_feat, t_w1, preferred_element_type=jnp.float32)).astype(
        jnp.bfloat16
    )
    t_embed = jnp.dot(t_hidden, t_w2, preferred_element_type=jnp.float32)
    onehot = (jnp.arange(class_table.shape[0], dtype=jnp.int32)[None, :] == labels[:, None]).astype(
        jnp.bfloat16
    )
    return t_embed + jnp.dot(onehot, class_table, preferred_element_type=jnp.float32)


def layer_norm(values):
    centre = jnp.mean(values, axis=-1, keepdims=True)
    spread = jnp.mean((values - centre) ** 2, axis=-1, keepdims=True)
    return (values - centre) * lax.rsqrt(spread + 1e-06)


MESH = pl.DeviceIdType.MESH
VMEM_LIMIT = 60 * 1024 * 1024


def vmem():
    return pl.BlockSpec(memory_space=pltpu.VMEM)


def anywhere():
    return pl.BlockSpec(memory_space=pl.ANY)


def greet(peers):
    barrier = pltpu.get_barrier_semaphore()
    for peer in peers:
        pl.semaphore_signal(barrier, inc=1, device_id=peer, device_id_type=MESH)
    pl.semaphore_wait(barrier, len(peers))


def remote(src, dst, send, recv, peer):
    return pltpu.make_async_remote_copy(
        src_ref=src, dst_ref=dst, send_sem=send, recv_sem=recv, device_id=peer, device_id_type=MESH
    )


def halo_kernel(n, x_ref, out_ref, got, send, recv):
    row = lax.axis_index("row")
    head = lax.axis_index("head")
    other = 1 - head
    above = lax.rem(row + n - 1, n)
    below = lax.rem(row + 1, n)
    plan = [
        ({"row": above}, 4),
        ({"row": above, "head": other}, 5),
        ({"head": other}, 3),
        ({"row": below}, 0),
        ({"row": below, "head": other}, 1),
    ]
    greet([peer for peer, _ in plan])
    copies = [
        remote(x_ref, got.at[slot], send.at[slot], recv.at[slot], peer) for peer, slot in plan
    ]
    for copy in copies:
        copy.start()
    for copy in copies:
        copy.wait()
    rows = x_ref.shape[1]

    def widened(same, opposite):
        left = jnp.where(head == 0, same, opposite)
        right = jnp.where(head == 0, opposite, same)
        return jnp.concatenate([left, right], axis=3)

    own = widened(x_ref[...], got[3])
    over = widened(got[0, :, rows - 1 :], got[1, :, rows - 1 :])
    under = widened(got[4, :, :1], got[5, :, :1])
    out_ref[:, 1 : rows + 1] = own
    out_ref[:, :1] = jnp.where(row == 0, own[:, :1], over)
    out_ref[:, rows + 1 :] = jnp.where(row == n - 1, own[:, rows - 1 :], under)


def halo_exchange(block, n):
    batch, rows, channels, cols = block.shape
    return pl.pallas_call(
        functools.partial(halo_kernel, n),
        out_shape=jax.ShapeDtypeStruct((batch, rows + 2, channels, 2 * cols), block.dtype),
        in_specs=[vmem()],
        out_specs=vmem(),
        scratch_shapes=[
            pltpu.VMEM((6,) + block.shape, block.dtype),
            pltpu.SemaphoreType.DMA((6,)),
            pltpu.SemaphoreType.DMA((6,)),
        ],
        compiler_params=pltpu.CompilerParams(collective_id=1, has_side_effects=True),
        name="halo",
    )(block)


def sums_kernel(n, s_ref, m_ref, s_out, m_out, s_got, m_got, s_send, s_recv, m_send, m_recv):
    row = lax.axis_index("row")
    peers = [{"row": lax.rem(row + k, n)} for k in range(1, n)]
    greet(peers)
    copies = []
    for k, peer in enumerate(peers):
        copies.append(remote(s_ref, s_got.at[k], s_send.at[k], s_recv.at[k], peer))
        copies.append(remote(m_ref, m_got.at[k], m_send.at[k], m_recv.at[k], peer))
    for copy in copies:
        copy.start()
    for copy in copies:
        copy.wait()
    stats = s_ref[...]
    parts = m_ref[...].astype(jnp.float32)
    for k in range(n - 1):
        stats = stats + s_got[k]
        parts = parts + m_got[k].astype(jnp.float32)
    s_out[...] = stats
    m_out[...] = parts


def row_sums(stats, parts, n):
    return pl.pallas_call(
        functools.partial(sums_kernel, n),
        out_shape=(
            jax.ShapeDtypeStruct(stats.shape, jnp.float32),
            jax.ShapeDtypeStruct(parts.shape, jnp.float32),
        ),
        in_specs=[vmem()] * 2,
        out_specs=(vmem(), vmem()),
        scratch_shapes=[
            pltpu.VMEM((n - 1,) + stats.shape, stats.dtype),
            pltpu.VMEM((n - 1,) + parts.shape, parts.dtype),
        ]
        + [pltpu.SemaphoreType.DMA((n - 1,))] * 4,
        compiler_params=pltpu.CompilerParams(collective_id=2, has_side_effects=True),
        name="row_sums",
    )(stats, parts)


def dot_nt(left, right):
    return lax.dot_general(left, right, (((1,), (1,)), ((), ())), preferred_element_type=jnp.float32)


def dot_nn(left, right):
    return jnp.dot(left, right, preferred_element_type=jnp.float32)


def attention_kernel(pieces, tok_ref, mod_ref, qkv_ref, ow_ref, far_ow_ref, *rest):
    stale = rest[:pieces]
    mid_ref, n2_ref = rest[pieces : pieces + 2]
    kv, q_ref, k_ref, v_ref, acc, part, got, l_sem, s_sem, r_sem, ps_sem, pr_sem = rest[pieces + 2 :]
    batch, tokens, local_width = q_ref.shape
    tile_rows, full_cols, width = tok_ref.shape[1:]
    half = full_cols // 2
    keys = stale[0].shape[2]
    row = lax.axis_index("row")
    head = lax.axis_index("head")
    twin = {"row": row + 1 - 2 * lax.rem(row, 2)}
    other = {"head": 1 - head}
    greet([twin, other])

    def stale_copies(b):
        copies = []
        for i in range(1, pieces):
            copies.append(
                pltpu.make_async_copy(
                    stale[i].at[:, b], kv.at[:, b, pl.ds((i - 1) * keys, keys)], l_sem.at[b, i]
                )
            )
        for i in range(pieces):
            copies.append(
                remote(
                    stale[i].at[:, b],
                    kv.at[:, b, pl.ds((pieces - 1 + i) * keys, keys)],
                    s_sem.at[b, i],
                    r_sem.at[b, i],
                    twin,
                )
            )
        return copies

    def part_copy(b):
        return remote(part.at[b], got.at[b], ps_sem.at[b], pr_sem.at[b], other)

    @pl.loop(0, batch)
    def _(b):
        for copy in stale_copies(b):
            copy.start()

    acc[...] = jnp.zeros_like(acc)
    scale = math.log2(math.e) / math.sqrt(HD)

    @pl.loop(0, batch)
    def _(b):
        mod = mod_ref[b]
        flat = tok_ref[b].astype(jnp.float32).reshape(tokens, width)
        rows_in = (layer_norm(flat) * (1.0 + mod[1:2]) + mod[0:1]).astype(jnp.bfloat16)
        q_ref[b] = (dot_nt(rows_in, qkv_ref[0]) * scale).astype(jnp.bfloat16)
        k_ref[b] = dot_nt(rows_in, qkv_ref[1]).astype(jnp.bfloat16)
        v_ref[b] = dot_nt(rows_in, qkv_ref[2]).astype(jnp.bfloat16)

    @pl.loop(0, batch)
    def _(b):
        for copy in stale_copies(b):
            copy.wait()
        for h in range(local_width // HD):
            low, high = h * HD, (h + 1) * HD
            first = low // 128 * 128
            last = min(-(-high // 128) * 128, local_width)
            lanes = lax.broadcasted_iota(jnp.int32, (1, last - first), 1) + first
            inside = (lanes >= low) & (lanes < high)
            keep = jnp.where(inside, 1.0, 0.0)
            query = q_ref[b, :, first:last] * keep.astype(jnp.bfloat16)
            fresh = dot_nt(query, k_ref[b, :, first:last])
            coarse = dot_nt(query, kv[0, b, :, first:last]) + 2.0
            top = jnp.maximum(
                jnp.max(fresh, axis=1, keepdims=True), jnp.max(coarse, axis=1, keepdims=True)
            )
            fresh = jnp.exp2(fresh - top)
            coarse = jnp.exp2(coarse - top)
            mass = jnp.sum(fresh, axis=1, keepdims=True) + jnp.sum(coarse, axis=1, keepdims=True)
            mixed = dot_nn(fresh.astype(jnp.bfloat16), v_ref[b, :, first:last]) + dot_nn(
                coarse.astype(jnp.bfloat16), kv[1, b, :, first:last]
            )
            mixed = mixed * (1.0 / mass)
            acc[:, first:last] = jnp.where(inside, mixed, acc[:, first:last])
        part[b] = acc[...].astype(jnp.bfloat16)
        part_copy(b).start()

    @pl.loop(0, batch)
    def _(b):
        part_copy(b).wait()
        total = dot_nn(part[b], ow_ref[...]) + dot_nn(got[b], far_ow_ref[...])
        mod = mod_ref[b]
        flat = tok_ref[b].astype(jnp.float32).reshape(tokens, width)
        mid = (flat + mod[2:3] * total).astype(jnp.bfloat16).astype(jnp.float32)
        normed = layer_norm(mid) * (1.0 + mod[4:5]) + mod[3:4]
        for ref, value in ((mid_ref, mid), (n2_ref, normed)):
            halves = value.astype(jnp.bfloat16).reshape(tile_rows, 2, half, width)
            ref[b, head] = halves[:, 0].reshape(tile_rows * half, width)
            ref[b, 1 - head] = halves[:, 1].reshape(tile_rows * half, width)


def attention_block(tokens, mod, qkv_w, out_w, far_out_w, stale):
    batch, tile_rows, full_cols, width = tokens.shape
    local_width = out_w.shape[0]
    per_image = tile_rows * full_cols
    mine = pltpu.VMEM((batch, per_image, local_width), jnp.bfloat16)
    pieces = len(stale)
    keys = stale[0].shape[2]
    half = full_cols // 2
    out = jax.ShapeDtypeStruct((batch, 2, tile_rows * half, width), jnp.bfloat16)
    return pl.pallas_call(
        functools.partial(attention_kernel, pieces),
        out_shape=(out, out),
        in_specs=[vmem()] * 5 + [anywhere()] * pieces,
        out_specs=(vmem(), vmem()),
        scratch_shapes=[
            pltpu.VMEM((2, batch, (2 * pieces - 1) * keys, local_width), jnp.bfloat16),
            mine,
            mine,
            mine,
            pltpu.VMEM((per_image, local_width), jnp.float32),
            mine,
            mine,
            pltpu.SemaphoreType.DMA((batch, pieces)),
            pltpu.SemaphoreType.DMA((batch, pieces)),
            pltpu.SemaphoreType.DMA((batch, pieces)),
            pltpu.SemaphoreType.DMA((batch,)),
            pltpu.SemaphoreType.DMA((batch,)),
        ],
        compiler_params=pltpu.CompilerParams(
            collective_id=3, has_side_effects=True, vmem_limit_bytes=VMEM_LIMIT
        ),
        name="attention",
    )(tokens, mod, qkv_w, out_w, far_out_w, *stale)


def mlp_kernel(far, n2_ref, mid_ref, mod_ref, up_ref, down_ref, *rest):
    ups = rest[:far]
    downs = rest[far : 2 * far]
    out_ref = rest[2 * far]
    ups_all, downs_all, own, part, got, ps, pr, wl, ws, wr = rest[2 * far + 1 :]
    batch, _, tokens, width = n2_ref.shape
    rows = ups[0].shape[0]
    row = lax.axis_index("row")
    core = lax.rem(row, 2)
    twin = {"row": row + 1 - 2 * core}
    other = {"head": 1 - lax.axis_index("head")}
    greet([twin, other])

    def part_copy(b):
        return remote(part.at[b], got.at[b], ps.at[b], pr.at[b], other)

    at = pl.ds(pl.multiple_of(core * rows, rows), rows)
    weight_copies = []
    for i in range(far):
        for j, (source, target) in enumerate(((ups[i], ups_all), (downs[i], downs_all))):
            place = target.at[i, at]
            weight_copies.append(pltpu.make_async_copy(source, place, wl.at[i, j]))
            weight_copies.append(remote(source, place, ws.at[i, j], wr.at[i, j], twin))

    for copy in weight_copies:
        copy.start()

    def mlp(rows_in, up, down):
        hidden = jax.nn.gelu(dot_nn(rows_in, up), approximate=True).astype(jnp.bfloat16)
        return dot_nt(hidden, down)

    def flat(half):
        return n2_ref[:, half].reshape(batch * tokens, width)

    own[...] = mlp(flat(1), up_ref[...], down_ref[...]).reshape(own.shape)
    for copy in weight_copies:
        copy.wait()

    @pl.loop(0, batch)
    def _(b):
        total = lax.fori_loop(
            0, far, lambda i, so_far: so_far + mlp(n2_ref[b, 1], ups_all[i], downs_all[i]), own[b]
        )
        part[b] = total.astype(jnp.bfloat16)
        part_copy(b).start()

    own[...] = mlp(flat(0), up_ref[...], down_ref[...]).reshape(own.shape)

    @pl.loop(0, far)
    def _(i):
        own[...] += mlp(flat(0), ups_all[i], downs_all[i]).reshape(own.shape)

    @pl.loop(0, batch)
    def _(b):
        part_copy(b).wait()
        total = own[b] + got[b].astype(jnp.float32)
        gate = mod_ref[b][5:6]
        out_ref[b] = (mid_ref[b, 0].astype(jnp.float32) + gate * total).astype(jnp.bfloat16)


def mlp_block(n2, mid, mod, up, down, ups, downs):
    far = len(ups)
    batch, _, tokens, width = n2.shape
    hidden = up.shape[1]
    shape = (batch, tokens, width)
    return pl.pallas_call(
        functools.partial(mlp_kernel, far),
        out_shape=jax.ShapeDtypeStruct(shape, jnp.bfloat16),
        in_specs=[vmem()] * 5 + [anywhere()] * (2 * far),
        out_specs=vmem(),
        scratch_shapes=[
            pltpu.VMEM((far, width, hidden), jnp.bfloat16),
            pltpu.VMEM((far, width, hidden), jnp.bfloat16),
            pltpu.VMEM(shape, jnp.float32),
            pltpu.VMEM(shape, jnp.bfloat16),
            pltpu.VMEM(shape, jnp.bfloat16),
        ]
        + [pltpu.SemaphoreType.DMA((batch,))] * 2
        + [pltpu.SemaphoreType.DMA((far, 2))] * 3,
        compiler_params=pltpu.CompilerParams(
            collective_id=4, has_side_effects=True, vmem_limit_bytes=VMEM_LIMIT
        ),
        name="mlp",
    )(n2, mid, mod, up, down, *ups, *downs)


def shifted(block, axis, step):
    count = lax.axis_size(axis)
    return lax.ppermute(block, axis, [(i, (i + step) % count) for i in range(count)])


def body(
    x_lo,
    noise,
    t_index,
    labels,
    stale_kv,
    embed_w,
    t_w1,
    t_w2,
    class_table,
    ada_w,
    qkv_w,
    out_w,
    fc1_w,
    fc2_w,
):
    row_index = lax.axis_index("row")
    row_count = lax.axis_size("row")
    head_index = lax.axis_index("head")
    head_count = lax.axis_size("head")
    batch = noise.shape[0]
    tile_rows = noise.shape[1]
    full_cols = noise.shape[2]
    channels = x_lo.shape[3]
    width = embed_w.shape[1]
    local_width = qkv_w.shape[2]
    half_cols = full_cols // head_count
    padded = halo_exchange(x_lo.transpose(0, 1, 3, 2), row_count).transpose(0, 1, 3, 2)
    stale_local = stale_kv.reshape(2, batch, -1, local_width)
    padded, stale_local, out_w = lax.optimization_barrier((padded, stale_local, out_w))
    far_out_w = shifted(out_w, "head", 1)
    stale = [stale_local]
    stale += [shifted(stale_local, "row", 2 * k) for k in range(1, row_count // 2)]
    core = lax.rem(row_index, 2)
    rows = fc1_w.shape[0] // 2
    up_half = lax.dynamic_slice_in_dim(fc1_w, core * rows, rows, 0)
    down_half = lax.dynamic_slice_in_dim(fc2_w, core * rows, rows, 0)
    ups = [shifted(up_half, "col", k) for k in range(1, lax.axis_size("col"))]
    downs = [shifted(down_half, "col", k) for k in range(1, lax.axis_size("col"))]
    abar = noise_level(t_index)
    padded = jnp.pad(padded, ((0, 0), (0, 0), (1, 1), (0, 0)), mode="edge")
    upsampled = upsample_padded(padded)
    noisy = (
        jnp.sqrt(abar)[:, None, None, None] * upsampled
        + jnp.sqrt(1.0 - abar)[:, None, None, None] * noise
    )
    grouped = noisy.reshape(batch, tile_rows, full_cols, 4, channels)
    cond_part = condition(t_index, labels, t_w1, t_w2, class_table)
    cond_act = jax.nn.silu(cond_part).astype(jnp.bfloat16)
    mod_part = jnp.dot(cond_act, ada_w, preferred_element_type=jnp.float32).astype(jnp.bfloat16)
    sums = jnp.concatenate(
        [
            jnp.sum(grouped, axis=(1, 2, 3)).reshape(-1),
            jnp.sum(grouped * grouped, axis=(1, 2, 3)).reshape(-1),
        ]
    )
    n_sums = sums.shape[0]
    sums = jnp.broadcast_to(jnp.pad(sums, (0, 128 - n_sums))[None], (8, 128))
    sums, modulation = row_sums(sums, mod_part.reshape(-1, 128), row_count)
    total, squares = sums[0, :n_sums].reshape(2, batch, channels)
    modulation = modulation.reshape(batch, 6, width)
    count = 4.0 * tile_rows * row_count * full_cols
    centre = total / count
    spread = squares / count - centre * centre
    normed = (
        (grouped - centre[:, None, None, None, :])
        * lax.rsqrt(spread + 1e-05)[:, None, None, None, :]
    ).reshape(batch, tile_rows, full_cols, 4 * channels)
    row_pos = (row_index * tile_rows + jnp.arange(tile_rows, dtype=jnp.int32)).astype(jnp.float32)
    col_pos = jnp.arange(full_cols, dtype=jnp.float32)
    pos = position_table(row_pos, col_pos, width)
    tokens = (
        jnp.einsum("bijf,fd->bijd", normed, embed_w, precision=lax.Precision.HIGHEST) + pos[None]
    ).astype(jnp.bfloat16)
    mid, normed2 = attention_block(
        tokens, modulation, qkv_w.transpose(1, 2, 0), out_w, far_out_w, stale
    )
    tokens_out = mlp_block(normed2, mid, modulation, fc1_w, fc2_w, ups, downs)
    return tokens_out.reshape(batch, tile_rows, half_cols, width)


def solution(mesh):
    placed = (
        P("col", "row", "head", None),
        P("col", "row", None, None),
        P("col"),
        P("col"),
        P(None, "col", "row", None, "head"),
        P(),
        P(),
        P(None, "row"),
        P(None, "row"),
        P("row", None),
        P(None, None, "head"),
        P("head", None),
        P(None, ("col", "head")),
        P(None, ("col", "head")),
    )
    return jax.shard_map(
        body, mesh=mesh, in_specs=placed, out_specs=P("col", "row", "head", None), check_vma=False
    )
```
